32 devices in a mesh: dp: 8 (over z, x), shard: 4 (over y, core).
Axes of the slice: x: 2, y: 2, z: 4, core: 2. Of those that a mesh axis runs over, the one named last changes fastest.
Arguments:
- grads: bfloat16 [8, 384, 8192], P('dp', 'shard'), may hold values from -6 to 6
- momentum: float32 [8, 384, 8192], P('dp', 'shard'), may hold values from -6 to 6
- param: float32 [384, 8192], P('shard'), may hold values from -6 to 6
- thresholds: float32 [384], P('shard'), may hold values from 0.1 to 1
- sel_blocks: int32 [8, 4, 768], P(None, 'shard'), may hold values from 0 to 6143, as said below
- counts: int32 [8, 4], P(None, 'shard'), may hold values from 192 to 768, as said below
Outputs:
- new_momentum: float32 [8, 384, 8192], P('dp', 'shard')
- new_param: float32 [384, 8192], P('shard')
- compute_copy: bfloat16 [384, 8192], replicated
The draws below stay inside these ranges and needn't reach their ends.
Inputs may be any that keep to these rules, and one draw needn't show every extreme that they name: `sel_blocks`: within one replica and shard the 768 entries are distinct block numbers of that shard. `counts`: some replica has 768 live slots in every shard.
All inputs are finite; a program needn't handle non-finite values.
Results may differ from the reference program's by a relative error of at most 0.0019.
Values may be sent and summed in bfloat16 or wider, within the bound.
A program may use at most 128 MiB of HBM per device.

```python
import math
import jax
import jax.numpy as jnp
from jax import lax

D = 8192
NBLK = 6144
KMAX = 768
REPLICAS = 8
SHARDS = 4
ROWS = 384


def place_value(block_row, target, slot):
    current = block_row[slot]
    block_row = jnp.where(block_row == target, current, block_row)
    return block_row.at[slot].set(target)


def fix_row(block_row):
    return place_value(place_value(block_row, NBLK - 1, 0), 0, 1)


def shuffle_one(one_key):
    return jax.random.permutation(one_key, NBLK)


def selection(key):
    base_key = jax.random.fold_in(key, 17)
    perm_keys = jax.random.split(jax.random.fold_in(base_key, 1), REPLICAS * SHARDS)
    shuffled = jax.vmap(shuffle_one)(perm_keys).astype(jnp.int32).reshape(REPLICAS, SHARDS, NBLK)
    hot_replica = jax.random.randint(jax.random.fold_in(base_key, 2), (), 0, REPLICAS)
    fixed_rows = jax.vmap(jax.vmap(fix_row))(shuffled)
    is_hot = (jnp.arange(REPLICAS, dtype=jnp.int32) == hot_replica)[:, None, None]
    block_lists = jnp.where(is_hot, fixed_rows, shuffled)[:, :, :KMAX].astype(jnp.int32)
    live_counts = jax.random.randint(jax.random.fold_in(base_key, 3), (REPLICAS, SHARDS), max(KMAX // 4, 1), KMAX + 1)
    live_counts = jnp.where(is_hot[:, :, 0], KMAX, live_counts).astype(jnp.int32)
    return (block_lists, live_counts)


def draw_sel_blocks(key, part):
    return selection(key)[0]


def draw_counts(key, part):
    return selection(key)[1]


def block_scale(stream_key, shape, cuts, least, top_value):
    loudness = 1.0
    for dim, blocks in cuts:
        draws = jax.random.uniform(jax.random.fold_in(jax.random.fold_in(stream_key, 6), dim), (blocks,), jnp.float32, least / len(cuts), top_value / len(cuts))
        loudness = loudness * jnp.repeat(jnp.exp(draws), shape[dim] // blocks).reshape((-1,) + (1,) * (len(shape) - 1 - dim))
    return loudness


def scatter_about(own_key, shape, spread, bound, shards=(), kind=jnp.bfloat16):
    loudness = block_scale(own_key, shape, shards, -0.22, 0.18) if shards else 1.0
    array = jax.random.normal(own_key, shape, jnp.float32) * spread * loudness
    return jnp.minimum(jnp.maximum(array, -bound), bound).astype(kind)


def setup_inputs(seed: int = 0) -> dict:
    streams_of = jax.random.split(jax.random.key(seed), 7)
    return {
        "grads": scatter_about(streams_of[0], (REPLICAS, ROWS, D), 1.0, 6.0, ((0, 8), (1, 4))),
        "momentum": scatter_about(streams_of[1], (REPLICAS, ROWS, D), 1.0, 6.0, ((0, 8), (1, 4)), jnp.float32),
        "param": scatter_about(streams_of[2], (ROWS, D), 1.0, 6.0, ((0, 4),), jnp.float32),
        "thresholds": jnp.clip(jnp.exp(math.log(1.0) - 2.3025851 * jax.random.uniform(streams_of[3], (ROWS,), jnp.float32) ** block_scale(streams_of[3], (ROWS,), ((0, 4),), -0.2, 0.2)), 0.1, 1.0),
        "sel_blocks": draw_sel_blocks(jax.random.fold_in(streams_of[6], 71), 0),
        "counts": draw_counts(jax.random.fold_in(streams_of[6], 71), 0),
    }


beta_decay = 0.999
step_size = 0.1

def dct_table():
    positions = jnp.arange(128, dtype=jnp.int32)
    sample = (positions % 64)[:, None]
    freq = (positions % 64)[None, :]
    same_half = positions[:, None] // 64 == positions[None, :] // 64
    weights = jnp.where(freq == 0, math.sqrt(1.0 / 64.0), math.sqrt(2.0 / 64.0)).astype(jnp.float32)
    angles = ((2 * sample + 1) * freq).astype(jnp.float32) * (math.pi / 128.0)
    return jnp.where(same_half, weights * jnp.cos(angles), 0.0).astype(jnp.float32)

def reference(grads, momentum, param, thresholds, sel_blocks, counts):
    table = dct_table()
    per_row = D // 128
    thr_blocks = jnp.repeat(thresholds, per_row)[:, None]
    slot_index = jnp.arange(KMAX, dtype=jnp.int32)
    shard_base = (jnp.arange(SHARDS, dtype=jnp.int32) * NBLK)[:, None]

    def one_replica(total, inputs):
        grad_rep, mom_rep, sel_rep, count_rep = inputs
        blended = beta_decay * mom_rep + grad_rep.astype(jnp.float32)
        coefficients = jnp.dot(blended.reshape(-1, 128), table, precision=lax.Precision.HIGHEST, preferred_element_type=jnp.float32)
        shrunk = coefficients - jnp.clip(coefficients, -thr_blocks, thr_blocks)
        global_ids = (sel_rep + shard_base).reshape(-1).astype(jnp.int32)
        live_slots = (slot_index[None, :] < count_rep[:, None]).reshape(-1)
        chosen = jnp.where(live_slots[:, None], shrunk[global_ids], 0.0).astype(jnp.bfloat16)
        chosen = lax.optimization_barrier(chosen).astype(jnp.float32)
        sparse_dense = jnp.zeros_like(coefficients).at[global_ids].add(chosen)
        decoded = jnp.dot(sparse_dense, table.T, precision=lax.Precision.HIGHEST, preferred_element_type=jnp.float32)
        return (total + sparse_dense, blended - decoded.reshape(blended.shape))
    start_total = jnp.zeros((ROWS * per_row, 128), jnp.float32)
    total, new_momentum = lax.scan(one_replica, start_total, (grads, momentum, sel_blocks, counts))
    averaged = total / REPLICAS
    direction = jnp.dot(averaged, table.T, precision=lax.Precision.HIGHEST, preferred_element_type=jnp.float32).reshape(param.shape)
    update = jnp.tanh(direction * lax.rsqrt(lax.optimization_barrier(jnp.mean(direction * direction, axis=1, keepdims=True)) + 1e-06))
    new_param = param - step_size * update
    return (new_momentum, new_param, new_param.astype(jnp.bfloat16))
```

```python
import functools

import jax
import jax.numpy as jnp
import numpy as np
from jax import lax
from jax.experimental import pallas as pl
from jax.experimental.pallas import tpu as pltpu
from jax.sharding import PartitionSpec as P

BLK = 128
HALF = 64
beta_decay = 0.999
step_size = 0.1
UNROLL = 16


def tables():
    pos = np.arange(BLK)
    sample, freq = (pos % HALF)[:, None], (pos % HALF)[None, :]
    same = pos[:, None] // HALF == pos[None, :] // HALF
    weights = np.where(freq == 0, np.sqrt(1.0 / HALF), np.sqrt(2.0 / HALF))
    table = np.where(same, weights * np.cos((2 * sample + 1) * freq * (np.pi / BLK)), 0.0).astype(np.float32)

    def wide(t):
        hi = t.astype(jnp.bfloat16)
        lo = (t - hi.astype(np.float32)).astype(jnp.bfloat16)
        half = np.concatenate([hi, lo], axis=1)
        return np.concatenate([half, half], axis=0)

    return wide(table), wide(table.T)


def split(x):
    hi = x.astype(jnp.bfloat16)
    lo = (x - hi.astype(jnp.float32)).astype(jnp.bfloat16)
    return jnp.concatenate([hi, lo], axis=1)


def both(x, w):
    y = jnp.dot(x, w, preferred_element_type=jnp.float32)
    return y[:, :BLK] + y[:, BLK:]


def tiles(x):
    return jnp.concatenate([x[:, c * BLK : (c + 1) * BLK] for c in range(x.shape[1] // BLK)], axis=0)


def encode_kernel(per_row, mom, grad, thr, sel, place, counts, fwd, inv, newmom, sent, rowhot, dense, picked):
    step = pl.program_id(0)
    replica = lax.axis_index("dp")
    rows, width = mom.shape
    slots = sel.shape[1]
    cols = width // BLK
    ids = sel[pl.ds(replica, 1), :]

    @pl.when(step == 0)
    def _():
        live = lax.broadcasted_iota(jnp.int32, (1, slots), 1) < counts[replica, 0]
        row_of = jnp.where(live, ids // per_row, -1)
        hot = row_of == lax.broadcasted_iota(jnp.int32, (rows, slots), 0)
        rowhot[...] = jnp.where(hot, 1.0, 0.0).astype(jnp.bfloat16)

    colhot = ids % per_row == step * cols + lax.broadcasted_iota(jnp.int32, (max(cols, 8), slots), 0)
    mask = lax.dot_general(
        rowhot[...],
        jnp.where(colhot, 1.0, 0.0).astype(jnp.bfloat16),
        (((1,), (1,)), ((), ())),
        preferred_element_type=jnp.float32,
    )
    blended = tiles(beta_decay * mom[...] + grad[...].astype(jnp.float32))
    coef = both(split(blended), fwd[...])
    t = jnp.concatenate([jnp.broadcast_to(thr[...], (rows, BLK))] * cols, axis=0)
    shrunk = coef - jnp.clip(coef, -t, t)
    keep = jnp.concatenate([jnp.broadcast_to(mask[:, c : c + 1], (rows, BLK)) for c in range(cols)], axis=0)
    kept = jnp.where(keep > 0.5, shrunk, 0.0)
    dense[pl.ds(pl.multiple_of(step * (cols * rows), 8), cols * rows), :] = kept
    out = blended - both(kept.astype(jnp.bfloat16), inv[:BLK, :])
    for c in range(cols):
        newmom[:, c * BLK : (c + 1) * BLK] = out[c * rows : (c + 1) * rows]

    @pl.when(step == pl.num_programs(0) - 1)
    def _():
        def pick(i, carry):
            base = i * UNROLL
            got = [dense[pl.ds(place[replica, base + u], 1), :] for u in range(UNROLL)]
            for u in range(UNROLL):
                picked[pl.ds(base + u, 1), :] = got[u]
            return carry

        lax.fori_loop(0, slots // UNROLL, pick, 0)
        sent[...] = picked[...].astype(jnp.bfloat16)


def encode(mom, grad, thr, sel, place, counts, fwd, inv, width):
    rows, D = mom.shape
    reps, slots = sel.shape
    col = pl.BlockSpec((rows, width), lambda i: (0, i))
    whole = lambda a: pl.BlockSpec(a.shape, lambda i: (0,) * a.ndim)
    smem = pl.BlockSpec(memory_space=pltpu.SMEM)
    return pl.pallas_call(
        functools.partial(encode_kernel, D // BLK),
        grid=(D // width,),
        in_specs=[col, col, whole(thr), whole(sel), smem, smem, whole(fwd), whole(inv)],
        out_specs=[col, pl.BlockSpec((slots, BLK), lambda i: (0, 0))],
        out_shape=[
            jax.ShapeDtypeStruct(mom.shape, jnp.float32),
            jax.ShapeDtypeStruct((slots, BLK), jnp.bfloat16),
        ],
        scratch_shapes=[
            pltpu.VMEM((rows, slots), jnp.bfloat16),
            pltpu.VMEM((rows * (D // BLK), BLK), jnp.float32),
            pltpu.VMEM((slots, BLK), jnp.float32),
        ],
        name="encode",
    )(mom, grad, thr, sel, place, counts, fwd, inv)


def apply_kernel(reps, place, sent, param, inv, newparam, copy, total, wide, scale):
    step = pl.program_id(0)
    rows, width = param.shape
    slots = wide.shape[0]
    cols = width // BLK
    all_cols = total.shape[0] // rows

    @pl.when(step == 0)
    def _():
        total[...] = jnp.zeros_like(total)

    @pl.when(step < reps)
    def _():
        wide[...] = sent[0].astype(jnp.float32)

        def put(i, carry):
            base = pl.multiple_of(i * UNROLL, UNROLL)
            at = [place[step, base + u] for u in range(UNROLL)]
            new = [total[pl.ds(at[u], 1), :] + wide[pl.ds(base + u, 1), :] for u in range(UNROLL)]
            for u in range(UNROLL):
                total[pl.ds(at[u], 1), :] = new[u]
            return carry

        lax.fori_loop(0, slots // UNROLL, put, 0)

    @pl.when(step == reps)
    def _():
        def square(c, acc):
            a = total[pl.ds(pl.multiple_of(c * rows, 8), rows), :] * (1.0 / reps)
            return acc + a * a

        acc = lax.fori_loop(0, all_cols, square, jnp.zeros((rows, BLK), jnp.float32), unroll=4)
        mean = jnp.sum(acc, axis=1, keepdims=True) * (1.0 / (all_cols * BLK))
        scale[...] = jnp.broadcast_to(lax.rsqrt(mean + 1e-06), scale.shape)

    @pl.when(step >= reps)
    def _():
        at = pl.multiple_of((step - reps) * (cols * rows), 8)
        averaged = total[pl.ds(at, cols * rows), :] * (1.0 / reps)
        direction = both(split(averaged), inv[...])
        for c in range(cols):
            lanes = slice(c * BLK, (c + 1) * BLK)
            update = jnp.tanh(direction[c * rows : (c + 1) * rows] * scale[...])
            new = param[:, lanes] - step_size * update
            newparam[:, lanes] = new
            copy[:, lanes] = new.astype(jnp.bfloat16)


def apply(place, sent, param, inv, width):
    rows, D = param.shape
    reps, slots, _ = sent.shape
    col = pl.BlockSpec((rows, width), lambda i: (0, jnp.maximum(i - reps, 0)))
    return pl.pallas_call(
        functools.partial(apply_kernel, reps),
        grid=(reps + D // width,),
        in_specs=[
            pl.BlockSpec(memory_space=pltpu.SMEM),
            pl.BlockSpec((1, slots, BLK), lambda i: (jnp.minimum(i, reps - 1), 0, 0)),
            col,
            pl.BlockSpec(inv.shape, lambda i: (0, 0)),
        ],
        out_specs=[col, col],
        out_shape=[
            jax.ShapeDtypeStruct(param.shape, jnp.float32),
            jax.ShapeDtypeStruct(param.shape, jnp.bfloat16),
        ],
        scratch_shapes=[
            pltpu.VMEM((rows * (D // BLK), BLK), jnp.float32),
            pltpu.VMEM((slots, BLK), jnp.float32),
            pltpu.VMEM((rows, BLK), jnp.float32),
        ],
        name="apply",
    )(place, sent, param, inv)


def on_device(grads, momentum, param, thresholds, sel_blocks, counts):
    rows, D = param.shape
    per_row = D // BLK
    width = min(1024, D)
    fwd, inv = (jnp.asarray(t) for t in tables())
    sel = sel_blocks[:, 0, :]
    place = (sel % per_row) * rows + sel // per_row
    new_momentum, sent = encode(
        momentum[0], grads[0], thresholds[:, None], sel, place, counts, fwd, inv, width
    )
    gathered = lax.all_gather(sent, "dp", axis=0, tiled=False)
    new_param, copy = apply(place, gathered, param, inv, width)
    compute_copy = lax.all_gather(copy, "shard", axis=0, tiled=True)
    return (new_momentum[None], new_param, compute_copy)


def solution(mesh):
    placed = (
        P("dp", "shard", None),
        P("dp", "shard", None),
        P("shard", None),
        P("shard"),
        P(None, "shard", None),
        P(None, "shard"),
    )
    return jax.shard_map(
        on_device,
        mesh=mesh,
        in_specs=placed,
        out_specs=(P("dp", "shard", None), P("shard", None), P()),
        check_vma=False,
    )
```

```python
import functools

import jax
import jax.numpy as jnp
import numpy as np
from jax import lax
from jax.experimental import pallas as pl
from jax.experimental.pallas import tpu as pltpu
from jax.sharding import PartitionSpec as P

BLK = 128
HALF = 64
beta_decay = 0.999
step_size = 0.1
UNROLL = 16


def tables():
    pos = np.arange(BLK)
    sample, freq = (pos % HALF)[:, None], (pos % HALF)[None, :]
    same = pos[:, None] // HALF == pos[None, :] // HALF
    weights = np.where(freq == 0, np.sqrt(1.0 / HALF), np.sqrt(2.0 / HALF))
    table = np.where(same, weights * np.cos((2 * sample + 1) * freq * (np.pi / BLK)), 0.0).astype(np.float32)

    def wide(t):
        hi = t.astype(jnp.bfloat16)
        lo = (t - hi.astype(np.float32)).astype(jnp.bfloat16)
        half = np.concatenate([hi, lo], axis=1)
        return np.concatenate([half, half], axis=0)

    return wide(table), wide(table.T)


def split(x):
    hi = x.astype(jnp.bfloat16)
    lo = (x - hi.astype(jnp.float32)).astype(jnp.bfloat16)
    return jnp.concatenate([hi, lo], axis=1)


def both(x, w):
    y = jnp.dot(x, w, preferred_element_type=jnp.float32)
    return y[:, :BLK] + y[:, BLK:]


def tiles(x):
    return jnp.concatenate([x[:, c * BLK : (c + 1) * BLK] for c in range(x.shape[1] // BLK)], axis=0)


def encode_kernel(per_row, mom, grad, thr, sel, place, counts, fwd, inv, newmom, sent, rowhot, dense, picked):
    step = pl.program_id(0)
    replica = lax.axis_index("dp")
    rows, width = mom.shape
    slots = sel.shape[1]
    cols = width // BLK
    ids = sel[pl.ds(replica, 1), :]

    @pl.when(step == 0)
    def _():
        live = lax.broadcasted_iota(jnp.int32, (1, slots), 1) < counts[replica, 0]
        row_of = jnp.where(live, ids // per_row, -1)
        hot = row_of == lax.broadcasted_iota(jnp.int32, (rows, slots), 0)
        rowhot[...] = jnp.where(hot, 1.0, 0.0).astype(jnp.bfloat16)

    colhot = ids % per_row == step * cols + lax.broadcasted_iota(jnp.int32, (max(cols, 8), slots), 0)
    mask = lax.dot_general(
        rowhot[...],
        jnp.where(colhot, 1.0, 0.0).astype(jnp.bfloat16),
        (((1,), (1,)), ((), ())),
        preferred_element_type=jnp.float32,
    )
    blended = tiles(beta_decay * mom[...] + grad[...].astype(jnp.float32))
    coef = both(split(blended), fwd[...])
    t = jnp.concatenate([jnp.broadcast_to(thr[...], (rows, BLK))] * cols, axis=0)
    shrunk = coef - jnp.clip(coef, -t, t)
    keep = jnp.concatenate([jnp.broadcast_to(mask[:, c : c + 1], (rows, BLK)) for c in range(cols)], axis=0)
    kept = jnp.where(keep > 0.5, shrunk, 0.0)
    dense[pl.ds(pl.multiple_of(step * (cols * rows), 8), cols * rows), :] = kept
    out = blended - both(kept.astype(jnp.bfloat16), inv[:BLK, :])
    for c in range(cols):
        newmom[:, c * BLK : (c + 1) * BLK] = out[c * rows : (c + 1) * rows]

    @pl.when(step == pl.num_programs(0) - 1)
    def _():
        def pick(i, carry):
            base = i * UNROLL
            got = [dense[pl.ds(place[replica, base + u], 1), :] for u in range(UNROLL)]
            for u in range(UNROLL):
                picked[pl.ds(base + u, 1), :] = got[u]
            return carry

        lax.fori_loop(0, slots // UNROLL, pick, 0)
        sent[...] = picked[...].astype(jnp.bfloat16)


def encode(mom, grad, thr, sel, place, counts, fwd, inv, width):
    rows, D = mom.shape
    reps, slots = sel.shape
    col = pl.BlockSpec((rows, width), lambda i: (0, i))
    whole = lambda a: pl.BlockSpec(a.shape, lambda i: (0,) * a.ndim)
    smem = pl.BlockSpec(memory_space=pltpu.SMEM)
    return pl.pallas_call(
        functools.partial(encode_kernel, D // BLK),
        grid=(D // width,),
        in_specs=[col, col, whole(thr), whole(sel), smem, smem, whole(fwd), whole(inv)],
        out_specs=[col, pl.BlockSpec((slots, BLK), lambda i: (0, 0))],
        out_shape=[
            jax.ShapeDtypeStruct(mom.shape, jnp.float32),
            jax.ShapeDtypeStruct((slots, BLK), jnp.bfloat16),
        ],
        scratch_shapes=[
            pltpu.VMEM((rows, slots), jnp.bfloat16),
            pltpu.VMEM((rows * (D // BLK), BLK), jnp.float32),
            pltpu.VMEM((slots, BLK), jnp.float32),
        ],
        name="encode",
    )(mom, grad, thr, sel, place, counts, fwd, inv)


def apply_kernel(reps, place, sent, param, inv, newparam, copy, total, wide, scale):
    step = pl.program_id(0)
    rows, width = param.shape
    slots = wide.shape[0]
    cols = width // BLK
    all_cols = total.shape[0] // rows

    @pl.when(step == 0)
    def _():
        total[...] = jnp.zeros_like(total)

    @pl.when(step < reps)
    def _():
        wide[...] = sent[0].astype(jnp.float32)

        def put(i, carry):
            base = pl.multiple_of(i * UNROLL, UNROLL)
            at = [place[step, base + u] for u in range(UNROLL)]
            new = [total[pl.ds(at[u], 1), :] + wide[pl.ds(base + u, 1), :] for u in range(UNROLL)]
            for u in range(UNROLL):
                total[pl.ds(at[u], 1), :] = new[u]
            return carry

        lax.fori_loop(0, slots // UNROLL, put, 0)

    @pl.when(step == reps)
    def _():
        def square(c, acc):
            a = total[pl.ds(pl.multiple_of(c * rows, 8), rows), :] * (1.0 / reps)
            return acc + a * a

        acc = lax.fori_loop(0, all_cols, square, jnp.zeros((rows, BLK), jnp.float32), unroll=4)
        mean = jnp.sum(acc, axis=1, keepdims=True) * (1.0 / (all_cols * BLK))
        scale[...] = jnp.broadcast_to(lax.rsqrt(mean + 1e-06), scale.shape)

    @pl.when(step >= reps)
    def _():
        at = pl.multiple_of((step - reps) * (cols * rows), 8)
        averaged = total[pl.ds(at, cols * rows), :] * (1.0 / reps)
        direction = both(split(averaged), inv[...])
        for c in range(cols):
            lanes = slice(c * BLK, (c + 1) * BLK)
            update = jnp.tanh(direction[c * rows : (c + 1) * rows] * scale[...])
            new = param[:, lanes] - step_size * update
            newparam[:, lanes] = new
            copy[:, lanes] = new.astype(jnp.bfloat16)


def apply(place, sent, param, inv, width):
    rows, D = param.shape
    reps, slots, _ = sent.shape
    col = pl.BlockSpec((rows, width), lambda i: (0, jnp.maximum(i - reps, 0)))
    return pl.pallas_call(
        functools.partial(apply_kernel, reps),
        grid=(reps + D // width,),
        in_specs=[
            pl.BlockSpec(memory_space=pltpu.SMEM),
            pl.BlockSpec((1, slots, BLK), lambda i: (jnp.minimum(i, reps - 1), 0, 0)),
            col,
            pl.BlockSpec(inv.shape, lambda i: (0, 0)),
        ],
        out_specs=[col, col],
        out_shape=[
            jax.ShapeDtypeStruct(param.shape, jnp.float32),
            jax.ShapeDtypeStruct(param.shape, jnp.bfloat16),
        ],
        scratch_shapes=[
            pltpu.VMEM((rows * (D // BLK), BLK), jnp.float32),
            pltpu.VMEM((slots, BLK), jnp.float32),
            pltpu.VMEM((rows, BLK), jnp.float32),
        ],
        name="apply",
    )(place, sent, param, inv)


MESH = pl.DeviceIdType.MESH


def copy_to(src, dst, send, recv, peer):
    return pltpu.make_async_remote_copy(
        src_ref=src, dst_ref=dst, send_sem=send, recv_sem=recv, device_id=peer, device_id_type=MESH
    )


def share_sent_kernel(reps, mine, out, send, recv, local):
    me = lax.axis_index("dp")
    line, side = me // 2, lax.rem(me, 2)
    length = reps // 2
    up, down, across = {"dp": me + 2}, {"dp": me - 2}, {"dp": me + 1 - 2 * side}
    has_up, has_down = line < length - 1, line > 0

    barrier = pltpu.get_barrier_semaphore()
    pl.semaphore_signal(barrier, inc=1, device_id=across, device_id_type=MESH)

    @pl.when(has_up)
    def _():
        pl.semaphore_signal(barrier, inc=1, device_id=up, device_id_type=MESH)

    @pl.when(has_down)
    def _():
        pl.semaphore_signal(barrier, inc=1, device_id=down, device_id_type=MESH)

    pl.semaphore_wait(barrier, 1 + jnp.where(has_up, 1, 0) + jnp.where(has_down, 1, 0))

    def block(i, way, peer, own=False):
        src = mine if own else out.at[i]
        return copy_to(src, out.at[i], send.at[i, way], recv.at[i], peer)

    for act in ("start", "wait_send"):
        begin = act == "start"
        if begin:
            keep = pltpu.make_async_copy(mine, out.at[me], local)
            keep.start()

        @pl.when(has_up)
        def _():
            getattr(block(me, 0, up, True), act)()

        @pl.when(has_down)
        def _():
            getattr(block(me, 1, down, True), act)()

        getattr(block(me, 2, across, True), act)()
        for d in range(1, length):

            @pl.when(line >= d)
            def _():
                i = me - 2 * d
                if begin:
                    block(i, 0, across).wait_recv()

                @pl.when(has_up)
                def _():
                    getattr(block(i, 0, up), act)()

                getattr(block(i, 2, across), act)()

            @pl.when(line + d < length)
            def _():
                i = me + 2 * d
                if begin:
                    block(i, 1, across).wait_recv()

                @pl.when(has_down)
                def _():
                    getattr(block(i, 1, down), act)()

                getattr(block(i, 2, across), act)()

        if begin:
            for k in range(length):
                block(2 * k + 1 - side, 2, across).wait_recv()
    keep.wait()


def share_sent(sent, reps):
    return pl.pallas_call(
        functools.partial(share_sent_kernel, reps),
        out_shape=jax.ShapeDtypeStruct((reps,) + sent.shape, sent.dtype),
        in_specs=[pl.BlockSpec(memory_space=pl.ANY)],
        out_specs=pl.BlockSpec(memory_space=pl.ANY),
        scratch_shapes=[
            pltpu.SemaphoreType.DMA((reps, 3)),
            pltpu.SemaphoreType.DMA((reps,)),
            pltpu.SemaphoreType.DMA,
        ],
        compiler_params=pltpu.CompilerParams(collective_id=0, has_side_effects=True),
        name="share_sent",
    )(sent)


PIECES = 8


def share_rows_kernel(shards, mine, out, send, recv, local):
    dp, s = lax.axis_index("dp"), lax.axis_index("shard")
    core, far = lax.rem(s, 2), s // 2
    group = shards // 2
    g = lax.rem(dp, 4)
    flip1 = lambda v: v + 1 - 2 * lax.rem(v, 2)
    flip2 = lambda v: v + 2 - 4 * lax.rem(v // 2, 2)
    width = mine.shape[1] // PIECES
    inner, side, deep = {"shard": flip1(s)}, {"dp": flip1(dp)}, {"dp": flip2(dp)}
    outer = [2 * lax.rem(far + k, group) + core for k in range(1, group)]

    barrier = pltpu.get_barrier_semaphore()
    for peer in [inner, side, deep] + [{"shard": o} for o in outer]:
        pl.semaphore_signal(barrier, inc=1, device_id=peer, device_id_type=MESH)
    pl.semaphore_wait(barrier, 3 + len(outer))

    lanes = lambda j: pl.ds(pl.multiple_of(j * width, BLK), width)

    def piece(o, j, way, peer):
        ref = out.at[o, :, lanes(j)]
        return copy_to(ref, ref, send.at[o, j, way], recv.at[o, j], peer)

    def own(j, k):
        return copy_to(
            mine.at[:, lanes(j)], out.at[s, :, lanes(j)], send.at[s, j, k], recv.at[s, j], {"shard": outer[k]}
        )

    sends = []

    def go(c):
        c.start()
        sends.append(c)

    for half in (0, 4):
        for k in range(len(outer)):
            go(own(g + half, k))
    go(copy_to(mine, out.at[s], send.at[s, 0, group], recv.at[s, PIECES], inner))
    keep = pltpu.make_async_copy(mine, out.at[s], local)
    keep.start()

    for half in (0, 4):
        for o in outer:
            j = g + half
            piece(o, j, 0, inner).wait_recv()
            go(piece(o, j, 0, side))
            go(piece(o, j, 1, deep))
            go(piece(o, j, 2, inner))
    a, b, c = flip1(g), flip2(g), flip2(flip1(g))
    for half in (0, 4):
        for o in outer:
            piece(o, a + half, 0, inner).wait_recv()
            if half == 0:
                go(piece(o, a + half, 1, deep))
            go(piece(o, a + half, 2, inner))
            piece(o, b + half, 0, inner).wait_recv()
            if half == 4:
                go(piece(o, b + half, 0, side))
            go(piece(o, b + half, 2, inner))
    for half in (0, 4):
        for o in outer:
            piece(o, c + half, 0, inner).wait_recv()
            go(piece(o, c + half, 2, inner))
    for o in outer:
        for j in range(PIECES):
            piece(flip1(o), j, 0, inner).wait_recv()
    other = flip1(s)
    copy_to(mine, out.at[other], send.at[other, 0, 0], recv.at[other, PIECES], inner).wait_recv()
    for x in sends:
        x.wait_send()
    keep.wait()


def share_rows(copy, shards):
    rows, D = copy.shape
    out = pl.pallas_call(
        functools.partial(share_rows_kernel, shards),
        out_shape=jax.ShapeDtypeStruct((shards, rows, D), copy.dtype),
        in_specs=[pl.BlockSpec(memory_space=pl.ANY)],
        out_specs=pl.BlockSpec(memory_space=pl.ANY),
        scratch_shapes=[
            pltpu.SemaphoreType.DMA((shards, PIECES, max(3, shards))),
            pltpu.SemaphoreType.DMA((shards, PIECES + 1)),
            pltpu.SemaphoreType.DMA,
        ],
        compiler_params=pltpu.CompilerParams(collective_id=1, has_side_effects=True),
        name="share_rows",
    )(copy)
    return out.reshape(shards * rows, D)


def on_device(grads, momentum, param, thresholds, sel_blocks, counts):
    rows, D = param.shape
    per_row = D // BLK
    width = min(1024, D)
    fwd, inv = (jnp.asarray(t) for t in tables())
    sel = sel_blocks[:, 0, :]
    place = (sel % per_row) * rows + sel // per_row
    new_momentum, sent = encode(
        momentum[0], grads[0], thresholds[:, None], sel, place, counts, fwd, inv, width
    )
    gathered = share_sent(sent, sel.shape[0])
    new_param, copy = apply(place, gathered, param, inv, width)
    compute_copy = share_rows(copy, lax.axis_size("shard"))
    return (new_momentum[None], new_param, compute_copy)


def solution(mesh):
    placed = (
        P("dp", "shard", None),
        P("dp", "shard", None),
        P("shard", None),
        P("shard"),
        P(None, "shard", None),
        P(None, "shard"),
    )
    return jax.shard_map(
        on_device,
        mesh=mesh,
        in_specs=placed,
        out_specs=(P("dp", "shard", None), P("shard", None), P()),
        check_vma=False,
    )
```

```python
import functools

import jax
import jax.numpy as jnp
import numpy as np
from jax import lax
from jax.experimental import pallas as pl
from jax.experimental.pallas import tpu as pltpu
from jax.sharding import PartitionSpec as P

BLK = 128
HALF = 64
beta_decay = 0.999
step_size = 0.1
UNROLL = 16


def tables():
    pos = np.arange(BLK)
    sample, freq = (pos % HALF)[:, None], (pos % HALF)[None, :]
    same = pos[:, None] // HALF == pos[None, :] // HALF
    weights = np.where(freq == 0, np.sqrt(1.0 / HALF), np.sqrt(2.0 / HALF))
    table = np.where(same, weights * np.cos((2 * sample + 1) * freq * (np.pi / BLK)), 0.0).astype(np.float32)

    def wide(t):
        hi = t.astype(jnp.bfloat16)
        lo = (t - hi.astype(np.float32)).astype(jnp.bfloat16)
        half = np.concatenate([hi, lo], axis=1)
        return np.concatenate([half, half], axis=0)

    return wide(table), wide(table.T)


def split(x):
    hi = x.astype(jnp.bfloat16)
    lo = (x - hi.astype(jnp.float32)).astype(jnp.bfloat16)
    return jnp.concatenate([hi, lo], axis=1)


def both(x, w):
    y = jnp.dot(x, w, preferred_element_type=jnp.float32)
    return y[:, :BLK] + y[:, BLK:]


def tiles(x):
    return jnp.concatenate([x[:, c * BLK : (c + 1) * BLK] for c in range(x.shape[1] // BLK)], axis=0)


def encode_kernel(per_row, mom, grad, thr, sel, place, counts, fwd, inv, newmom, sent, rowhot, dense, picked, level):
    step = pl.program_id(0)
    replica = lax.axis_index("dp")
    rows, width = mom.shape
    slots = sel.shape[2]
    cols = width // BLK
    ids = sel[replica]

    @pl.when(step == 0)
    def _():
        live = lax.broadcasted_iota(jnp.int32, (1, slots), 1) < counts[replica]
        row_of = jnp.where(live, ids // per_row, -1)
        hot = row_of == lax.broadcasted_iota(jnp.int32, (rows, slots), 0)
        rowhot[...] = jnp.where(hot, 1.0, 0.0).astype(jnp.bfloat16)
        eye = lax.broadcasted_iota(jnp.int32, (rows, rows), 0) == lax.broadcasted_iota(jnp.int32, (rows, rows), 1)
        column = jnp.sum(jnp.where(eye, thr[...], 0.0), axis=1, keepdims=True)
        level[...] = jnp.broadcast_to(column, level.shape)

    colhot = ids % per_row == step * cols + lax.broadcasted_iota(jnp.int32, (max(cols, 8), slots), 0)
    mask = lax.dot_general(
        rowhot[...],
        jnp.where(colhot, 1.0, 0.0).astype(jnp.bfloat16),
        (((1,), (1,)), ((), ())),
        preferred_element_type=jnp.float32,
    )
    blended = tiles(beta_decay * mom[...] + grad[...].astype(jnp.float32))
    coef = both(split(blended), fwd[...])
    t = jnp.concatenate([level[...]] * cols, axis=0)
    shrunk = coef - jnp.clip(coef, -t, t)
    keep = jnp.concatenate([jnp.broadcast_to(mask[:, c : c + 1], (rows, BLK)) for c in range(cols)], axis=0)
    kept = jnp.where(keep > 0.5, shrunk, 0.0)
    for c in range(cols):
        dense[pl.ds(step * cols + c, rows, stride=per_row), :] = kept[c * rows : (c + 1) * rows]
    out = blended - both(kept.astype(jnp.bfloat16), inv[:BLK, :])
    for c in range(cols):
        newmom[:, c * BLK : (c + 1) * BLK] = out[c * rows : (c + 1) * rows]

    @pl.when(step == pl.num_programs(0) - 1)
    def _():
        def pick(i, carry):
            base = i * UNROLL
            got = [dense[pl.ds(place[replica, 0, base + u], 1), :] for u in range(UNROLL)]
            for u in range(UNROLL):
                picked[pl.ds(base + u, 1), :] = got[u]
            return carry

        lax.fori_loop(0, slots // UNROLL, pick, 0)
        sent[...] = picked[...].astype(jnp.bfloat16)


def encode(mom, grad, thr, sel, counts, fwd, inv, width):
    rows, D = mom.shape
    slots = sel.shape[2]
    col = pl.BlockSpec((rows, width), lambda i: (0, i))
    whole = lambda a: pl.BlockSpec(a.shape, lambda i: (0,) * a.ndim)
    smem = pl.BlockSpec(memory_space=pltpu.SMEM)
    return pl.pallas_call(
        functools.partial(encode_kernel, D // BLK),
        grid=(D // width,),
        in_specs=[col, col, whole(thr), whole(sel), smem, smem, whole(fwd), whole(inv)],
        out_specs=[col, pl.BlockSpec((slots, BLK), lambda i: (0, 0))],
        out_shape=[
            jax.ShapeDtypeStruct(mom.shape, jnp.float32),
            jax.ShapeDtypeStruct((slots, BLK), jnp.bfloat16),
        ],
        scratch_shapes=[
            pltpu.VMEM((rows, slots), jnp.bfloat16),
            pltpu.VMEM((rows * (D // BLK), BLK), jnp.float32),
            pltpu.VMEM((slots, BLK), jnp.float32),
            pltpu.VMEM((rows, BLK), jnp.float32),
        ],
        name="encode",
    )(mom, grad, thr, sel, sel, counts, fwd, inv)


def apply_kernel(reps, place, sent, param, inv, newparam, copy, total, wide, scale):
    step = pl.program_id(0)
    rows, width = param.shape
    slots = wide.shape[0]
    cols = width // BLK
    all_cols = total.shape[0] // rows

    @pl.when(step == 0)
    def _():
        total[...] = jnp.zeros_like(total)

    @pl.when(step < reps)
    def _():
        wide[...] = sent[0].astype(jnp.float32)

        def put(i, carry):
            base = pl.multiple_of(i * UNROLL, UNROLL)
            at = [place[step, 0, base + u] for u in range(UNROLL)]
            new = [total[pl.ds(at[u], 1), :] + wide[pl.ds(base + u, 1), :] for u in range(UNROLL)]
            for u in range(UNROLL):
                total[pl.ds(at[u], 1), :] = new[u]
            return carry

        lax.fori_loop(0, slots // UNROLL, put, 0)

    @pl.when(step == reps)
    def _():
        def square(c, acc):
            a = total[pl.ds(c, rows, stride=all_cols), :] * (1.0 / reps)
            return acc + a * a

        acc = lax.fori_loop(0, all_cols, square, jnp.zeros((rows, BLK), jnp.float32), unroll=4)
        mean = jnp.sum(acc, axis=1, keepdims=True) * (1.0 / (all_cols * BLK))
        scale[...] = jnp.broadcast_to(lax.rsqrt(mean + 1e-06), scale.shape)

    @pl.when(step >= reps)
    def _():
        first = (step - reps) * cols
        averaged = jnp.concatenate(
            [total[pl.ds(first + c, rows, stride=all_cols), :] for c in range(cols)], axis=0
        ) * (1.0 / reps)
        direction = both(split(averaged), inv[...])
        for c in range(cols):
            lanes = slice(c * BLK, (c + 1) * BLK)
            update = jnp.tanh(direction[c * rows : (c + 1) * rows] * scale[...])
            new = param[:, lanes] - step_size * update
            newparam[:, lanes] = new
            copy[:, lanes] = new.astype(jnp.bfloat16)


def apply(place, sent, param, inv, width):
    rows, D = param.shape
    reps, slots, _ = sent.shape
    col = pl.BlockSpec((rows, width), lambda i: (0, jnp.maximum(i - reps, 0)))
    return pl.pallas_call(
        functools.partial(apply_kernel, reps),
        grid=(reps + D // width,),
        in_specs=[
            pl.BlockSpec(memory_space=pltpu.SMEM),
            pl.BlockSpec((1, slots, BLK), lambda i: (jnp.minimum(i, reps - 1), 0, 0)),
            col,
            pl.BlockSpec(inv.shape, lambda i: (0, 0)),
        ],
        out_specs=[col, col],
        out_shape=[
            jax.ShapeDtypeStruct(param.shape, jnp.float32),
            jax.ShapeDtypeStruct(param.shape, jnp.bfloat16),
        ],
        scratch_shapes=[
            pltpu.VMEM((rows * (D // BLK), BLK), jnp.float32),
            pltpu.VMEM((slots, BLK), jnp.float32),
            pltpu.VMEM((rows, BLK), jnp.float32),
        ],
        name="apply",
    )(place, sent, param, inv)


MESH = pl.DeviceIdType.MESH


def copy_to(src, dst, send, recv, peer):
    return pltpu.make_async_remote_copy(
        src_ref=src, dst_ref=dst, send_sem=send, recv_sem=recv, device_id=peer, device_id_type=MESH
    )


def share_sent_kernel(reps, mine, out, send, recv, local):
    me = lax.axis_index("dp")
    line, side = me // 2, lax.rem(me, 2)
    length = reps // 2
    up, down, across = {"dp": me + 2}, {"dp": me - 2}, {"dp": me + 1 - 2 * side}
    has_up, has_down = line < length - 1, line > 0

    barrier = pltpu.get_barrier_semaphore()
    pl.semaphore_signal(barrier, inc=1, device_id=across, device_id_type=MESH)

    @pl.when(has_up)
    def _():
        pl.semaphore_signal(barrier, inc=1, device_id=up, device_id_type=MESH)

    @pl.when(has_down)
    def _():
        pl.semaphore_signal(barrier, inc=1, device_id=down, device_id_type=MESH)

    pl.semaphore_wait(barrier, 1 + jnp.where(has_up, 1, 0) + jnp.where(has_down, 1, 0))

    def block(i, way, peer, own=False):
        src = mine if own else out.at[i]
        return copy_to(src, out.at[i], send.at[i, way], recv.at[i], peer)

    for act in ("start", "wait_send"):
        begin = act == "start"
        if begin:
            keep = pltpu.make_async_copy(mine, out.at[me], local)
            keep.start()

        @pl.when(has_up)
        def _():
            getattr(block(me, 0, up, True), act)()

        @pl.when(has_down)
        def _():
            getattr(block(me, 1, down, True), act)()

        getattr(block(me, 2, across, True), act)()
        for d in range(1, length):

            @pl.when(line >= d)
            def _():
                i = me - 2 * d
                if begin:
                    block(i, 0, across).wait_recv()

                @pl.when(has_up)
                def _():
                    getattr(block(i, 0, up), act)()

                getattr(block(i, 2, across), act)()

            @pl.when(line + d < length)
            def _():
                i = me + 2 * d
                if begin:
                    block(i, 1, across).wait_recv()

                @pl.when(has_down)
                def _():
                    getattr(block(i, 1, down), act)()

                getattr(block(i, 2, across), act)()

        if begin:
            for k in range(length):
                block(2 * k + 1 - side, 2, across).wait_recv()
    keep.wait()


def share_sent(sent, reps):
    return pl.pallas_call(
        functools.partial(share_sent_kernel, reps),
        out_shape=jax.ShapeDtypeStruct((reps,) + sent.shape, sent.dtype),
        in_specs=[pl.BlockSpec(memory_space=pltpu.VMEM)],
        out_specs=pl.BlockSpec(memory_space=pl.ANY),
        scratch_shapes=[
            pltpu.SemaphoreType.DMA((reps, 3)),
            pltpu.SemaphoreType.DMA((reps,)),
            pltpu.SemaphoreType.DMA,
        ],
        compiler_params=pltpu.CompilerParams(collective_id=0, has_side_effects=True),
        name="share_sent",
    )(sent)


PIECES = 8


def share_rows_kernel(shards, mine, out, send, recv, local):
    dp, s = lax.axis_index("dp"), lax.axis_index("shard")
    core, far = lax.rem(s, 2), s // 2
    group = shards // 2
    g = lax.rem(dp, 4)
    flip1 = lambda v: v + 1 - 2 * lax.rem(v, 2)
    flip2 = lambda v: v + 2 - 4 * lax.rem(v // 2, 2)
    width = mine.shape[1] // PIECES
    inner, side, deep = {"shard": flip1(s)}, {"dp": flip1(dp)}, {"dp": flip2(dp)}
    outer = [2 * lax.rem(far + k, group) + core for k in range(1, group)]

    barrier = pltpu.get_barrier_semaphore()
    for peer in [inner, side, deep] + [{"shard": o} for o in outer]:
        pl.semaphore_signal(barrier, inc=1, device_id=peer, device_id_type=MESH)
    pl.semaphore_wait(barrier, 3 + len(outer))

    lanes = lambda j: pl.ds(pl.multiple_of(j * width, BLK), width)

    def piece(o, j, way, peer):
        ref = out.at[o, :, lanes(j)]
        return copy_to(ref, ref, send.at[o, j, way], recv.at[o, j], peer)

    def own(j, k):
        return copy_to(
            mine.at[:, lanes(j)], out.at[s, :, lanes(j)], send.at[s, j, k], recv.at[s, j], {"shard": outer[k]}
        )

    sends = []

    def go(c):
        c.start()
        sends.append(c)

    for half in (0, 4):
        for k in range(len(outer)):
            go(own(g + half, k))
    go(copy_to(mine, out.at[s], send.at[s, 0, group], recv.at[s, PIECES], inner))
    keep = pltpu.make_async_copy(mine, out.at[s], local)
    keep.start()

    for half in (0, 4):
        for o in outer:
            j = g + half
            piece(o, j, 0, inner).wait_recv()
            go(piece(o, j, 0, side))
            go(piece(o, j, 1, deep))
            go(piece(o, j, 2, inner))
    a, b, c = flip1(g), flip2(g), flip2(flip1(g))
    for half in (0, 4):
        for o in outer:
            piece(o, a + half, 0, inner).wait_recv()
            if half == 0:
                go(piece(o, a + half, 1, deep))
            go(piece(o, a + half, 2, inner))
            piece(o, b + half, 0, inner).wait_recv()
            if half == 4:
                go(piece(o, b + half, 0, side))
            go(piece(o, b + half, 2, inner))
    for half in (0, 4):
        for o in outer:
            piece(o, c + half, 0, inner).wait_recv()
            go(piece(o, c + half, 2, inner))
    for o in outer:
        for j in range(PIECES):
            piece(flip1(o), j, 0, inner).wait_recv()
    other = flip1(s)
    copy_to(mine, out.at[other], send.at[other, 0, 0], recv.at[other, PIECES], inner).wait_recv()
    for x in sends:
        x.wait_send()
    keep.wait()


def share_rows(copy, shards):
    rows, D = copy.shape
    out = pl.pallas_call(
        functools.partial(share_rows_kernel, shards),
        out_shape=jax.ShapeDtypeStruct((shards, rows, D), copy.dtype),
        in_specs=[pl.BlockSpec(memory_space=pltpu.VMEM)],
        out_specs=pl.BlockSpec(memory_space=pl.ANY),
        scratch_shapes=[
            pltpu.SemaphoreType.DMA((shards, PIECES, max(3, shards))),
            pltpu.SemaphoreType.DMA((shards, PIECES + 1)),
            pltpu.SemaphoreType.DMA,
        ],
        compiler_params=pltpu.CompilerParams(collective_id=1, has_side_effects=True),
        name="share_rows",
    )(copy)
    return out.reshape(shards * rows, D)


def on_device(grads, momentum, param, thresholds, sel_blocks, counts):
    rows, D = param.shape
    width = min(1024, D)
    fwd, inv = (jnp.asarray(t) for t in tables())
    new_momentum, sent = encode(
        momentum[0], grads[0], thresholds[None, :], sel_blocks, counts[:, 0], fwd, inv, width
    )
    gathered = share_sent(sent, sel_blocks.shape[0])
    new_param, copy = apply(sel_blocks, gathered, param, inv, width)
    compute_copy = share_rows(copy, lax.axis_size("shard"))
    return (new_momentum[None], new_param, compute_copy)


def solution(mesh):
    placed = (
        P("dp", "shard", None),
        P("dp", "shard", None),
        P("shard", None),
        P("shard"),
        P(None, "shard", None),
        P(None, "shard"),
    )
    return jax.shard_map(
        on_device,
        mesh=mesh,
        in_specs=placed,
        out_specs=(P("dp", "shard", None), P("shard", None), P()),
        check_vma=False,
    )
```

```python
import functools

import jax
import jax.numpy as jnp
import numpy as np
from jax import lax
from jax.experimental import pallas as pl
from jax.experimental.pallas import tpu as pltpu
from jax.sharding import PartitionSpec as P

BLK = 128
HALF = 64
beta_decay = 0.999
step_size = 0.1
UNROLL = 16


def tables():
    pos = np.arange(BLK)
    sample, freq = (pos % HALF)[:, None], (pos % HALF)[None, :]
    same = pos[:, None] // HALF == pos[None, :] // HALF
    weights = np.where(freq == 0, np.sqrt(1.0 / HALF), np.sqrt(2.0 / HALF))
    table = np.where(same, weights * np.cos((2 * sample + 1) * freq * (np.pi / BLK)), 0.0).astype(np.float32)

    def wide(t):
        hi = t.astype(jnp.bfloat16)
        lo = (t - hi.astype(np.float32)).astype(jnp.bfloat16)
        half = np.concatenate([hi, lo], axis=1)
        return np.concatenate([half, half], axis=0)

    return wide(table), wide(table.T)


def split(x):
    hi = x.astype(jnp.bfloat16)
    lo = (x - hi.astype(jnp.float32)).astype(jnp.bfloat16)
    return jnp.concatenate([hi, lo], axis=1)


def both(x, w):
    y = jnp.dot(x, w, preferred_element_type=jnp.float32)
    return y[:, :BLK] + y[:, BLK:]


def tiles(x):
    return jnp.concatenate([x[:, c * BLK : (c + 1) * BLK] for c in range(x.shape[1] // BLK)], axis=0)


def encode_kernel(per_row, mom, grad, thr, sel, place, counts, fwd, inv, newmom, sent, rowhot, dense, picked, level):
    step = pl.program_id(0)
    replica = lax.axis_index("dp")
    rows, width = mom.shape
    slots = sel.shape[2]
    cols = width // BLK
    ids = sel[replica]

    @pl.when(step == 0)
    def _():
        live = lax.broadcasted_iota(jnp.int32, (1, slots), 1) < counts[replica]
        row_of = jnp.where(live, ids // per_row, -1)
        hot = row_of == lax.broadcasted_iota(jnp.int32, (rows, slots), 0)
        rowhot[...] = jnp.where(hot, 1.0, 0.0).astype(jnp.bfloat16)
        eye = lax.broadcasted_iota(jnp.int32, (rows, rows), 0) == lax.broadcasted_iota(jnp.int32, (rows, rows), 1)
        column = jnp.sum(jnp.where(eye, thr[...], 0.0), axis=1, keepdims=True)
        level[...] = jnp.broadcast_to(column, level.shape)

    colhot = ids % per_row == step * cols + lax.broadcasted_iota(jnp.int32, (max(cols, 8), slots), 0)
    mask = lax.dot_general(
        rowhot[...],
        jnp.where(colhot, 1.0, 0.0).astype(jnp.bfloat16),
        (((1,), (1,)), ((), ())),
        preferred_element_type=jnp.float32,
    )
    blended = tiles(beta_decay * mom[...] + grad[...].astype(jnp.float32))
    coef = both(split(blended), fwd[...])
    t = jnp.concatenate([level[...]] * cols, axis=0)
    shrunk = coef - jnp.clip(coef, -t, t)
    keep = jnp.concatenate([jnp.broadcast_to(mask[:, c : c + 1], (rows, BLK)) for c in range(cols)], axis=0)
    kept = jnp.where(keep > 0.5, shrunk, 0.0)
    for c in range(cols):
        dense[pl.ds(step * cols + c, rows, stride=per_row), :] = kept[c * rows : (c + 1) * rows]
    out = blended - both(kept.astype(jnp.bfloat16), inv[:BLK, :])
    for c in range(cols):
        newmom[:, c * BLK : (c + 1) * BLK] = out[c * rows : (c + 1) * rows]

    @pl.when(step == pl.num_programs(0) - 1)
    def _():
        def pick(i, carry):
            base = i * UNROLL
            got = [dense[pl.ds(place[replica, 0, base + u], 1), :] for u in range(UNROLL)]
            for u in range(UNROLL):
                picked[pl.ds(base + u, 1), :] = got[u]
            return carry

        lax.fori_loop(0, slots // UNROLL, pick, 0)
        sent[...] = picked[...].astype(jnp.bfloat16)


def encode(mom, grad, thr, sel, counts, fwd, inv, width):
    rows, D = mom.shape
    slots = sel.shape[2]
    col = pl.BlockSpec((rows, width), lambda i: (0, i))
    whole = lambda a: pl.BlockSpec(a.shape, lambda i: (0,) * a.ndim)
    smem = pl.BlockSpec(memory_space=pltpu.SMEM)
    return pl.pallas_call(
        functools.partial(encode_kernel, D // BLK),
        grid=(D // width,),
        in_specs=[col, col, whole(thr), whole(sel), smem, smem, whole(fwd), whole(inv)],
        out_specs=[col, pl.BlockSpec((slots, BLK), lambda i: (0, 0))],
        out_shape=[
            jax.ShapeDtypeStruct(mom.shape, jnp.float32),
            jax.ShapeDtypeStruct((slots, BLK), jnp.bfloat16),
        ],
        scratch_shapes=[
            pltpu.VMEM((rows, slots), jnp.bfloat16),
            pltpu.VMEM((rows * (D // BLK), BLK), jnp.float32),
            pltpu.VMEM((slots, BLK), jnp.float32),
            pltpu.VMEM((rows, BLK), jnp.float32),
        ],
        name="encode",
    )(mom, grad, thr, sel, sel, counts, fwd, inv)


def apply_kernel(total, scale, param, inv, newparam, copy):
    rows, width = param.shape
    cols = width // BLK
    direction = both(split(tiles(total[...])), inv[...])
    for c in range(cols):
        lanes = slice(c * BLK, (c + 1) * BLK)
        update = jnp.tanh(direction[c * rows : (c + 1) * rows] * scale[...])
        new = param[:, lanes] - step_size * update
        newparam[:, lanes] = new
        copy[:, lanes] = new.astype(jnp.bfloat16)


def apply(total, scale, param, inv, width):
    rows, D = param.shape
    col = pl.BlockSpec((rows, width), lambda i: (0, i))
    whole = lambda a: pl.BlockSpec(a.shape, lambda i: (0,) * a.ndim)
    return pl.pallas_call(
        apply_kernel,
        grid=(D // width,),
        in_specs=[col, whole(scale), col, whole(inv)],
        out_specs=[col, col],
        out_shape=[
            jax.ShapeDtypeStruct(param.shape, jnp.float32),
            jax.ShapeDtypeStruct(param.shape, jnp.bfloat16),
        ],
        name="apply",
    )(total, scale, param, inv)


MESH = pl.DeviceIdType.MESH


def copy_to(src, dst, send, recv, peer):
    return pltpu.make_async_remote_copy(
        src_ref=src, dst_ref=dst, send_sem=send, recv_sem=recv, device_id=peer, device_id_type=MESH
    )


def sum_sent_kernel(reps, mine, sel, total, scale, buf, send, recv):
    me = lax.axis_index("dp")
    line, side = me // 2, lax.rem(me, 2)
    length = reps // 2
    rows, D = total.shape
    per_row = D // BLK
    slots = mine.shape[0]
    up, down, across = {"dp": me + 2}, {"dp": me - 2}, {"dp": me + 1 - 2 * side}
    has_up, has_down = line < length - 1, line > 0

    barrier = pltpu.get_barrier_semaphore()
    pl.semaphore_signal(barrier, inc=1, device_id=across, device_id_type=MESH)

    @pl.when(has_up)
    def _():
        pl.semaphore_signal(barrier, inc=1, device_id=up, device_id_type=MESH)

    @pl.when(has_down)
    def _():
        pl.semaphore_signal(barrier, inc=1, device_id=down, device_id_type=MESH)

    pl.semaphore_wait(barrier, 1 + jnp.where(has_up, 1, 0) + jnp.where(has_down, 1, 0))

    def block(i, way, peer, own=False):
        src = mine if own else buf.at[i]
        return copy_to(src, buf.at[i], send.at[i, way], recv.at[i], peer)

    def first(act):
        @pl.when(has_up)
        def _():
            getattr(block(me, 0, up, True), act)()

        @pl.when(has_down)
        def _():
            getattr(block(me, 1, down, True), act)()

        getattr(block(me, 2, across, True), act)()

    def relay(d, act):
        @pl.when(line >= d)
        def _():
            i = me - 2 * d
            if act == "start":
                block(i, 0, across).wait_recv()

            @pl.when(has_up)
            def _():
                getattr(block(i, 0, up), act)()

            getattr(block(i, 2, across), act)()

        @pl.when(line + d < length)
        def _():
            i = me + 2 * d
            if act == "start":
                block(i, 1, across).wait_recv()

            @pl.when(has_down)
            def _():
                getattr(block(i, 1, down), act)()

            getattr(block(i, 2, across), act)()

    first("start")
    total[...] = jnp.zeros_like(total)
    group = min(8, per_row // 2)

    def accumulate(i):
        ids = sel[i]
        col = ids % per_row
        hot = ids // per_row == lax.broadcasted_iota(jnp.int32, (rows, slots), 0)
        rowhot = jnp.where(hot, 1.0, 0.0).astype(jnp.bfloat16)
        odd = jnp.transpose(jnp.broadcast_to((col % 2).astype(jnp.float32), (BLK, slots)))
        right = odd.astype(jnp.bfloat16)
        values = buf[i]
        rhs = jnp.concatenate([values * (1.0 - odd).astype(jnp.bfloat16), values * right], axis=1)
        pair = jnp.broadcast_to(col // 2, (16, slots))

        def chunk(q, carry):
            parts = []
            for u in range(group):
                pick = jnp.where(pair == q * group + u, 1.0, 0.0).astype(jnp.bfloat16)
                parts.append(rowhot * jnp.concatenate([pick] * (rows // 16), axis=0))
            out = jnp.dot(jnp.concatenate(parts, axis=0), rhs, preferred_element_type=jnp.float32)
            for u in range(group):
                at = pl.ds(pl.multiple_of((q * group + u) * (2 * BLK), BLK), 2 * BLK)
                total[:, at] += out[u * rows : (u + 1) * rows]
            return carry

        lax.fori_loop(0, per_row // 2 // group, chunk, 0)

    buf[me] = mine[...]

    def step(d, carry):
        @pl.when(d > 0)
        def _():
            relay(d, "start")

        def visit(t, carry):
            other = t // 2
            far = d - other
            at = line + (2 * lax.rem(t, 2) - 1) * far
            twin = (far == 0) & (lax.rem(t, 2) == 1)

            @pl.when((far >= 0) & (at >= 0) & (at < length) & jnp.logical_not(twin))
            def _():
                i = 2 * at + side + other * (1 - 2 * side)

                @pl.when(other == 1)
                def _():
                    block(i, 2, across).wait_recv()

                accumulate(i)

            return carry

        lax.fori_loop(0, 4, visit, 0)
        return carry

    lax.fori_loop(0, length + 1, step, 0)
    first("wait_send")

    def drain(d, carry):
        relay(d, "wait_send")
        return carry

    lax.fori_loop(1, length, drain, 0)

    def square(c, acc):
        lanes = pl.ds(pl.multiple_of(c * BLK, BLK), BLK)
        a = total[:, lanes] * (1.0 / reps)
        total[:, lanes] = a
        return acc + a * a

    acc = lax.fori_loop(0, per_row, square, jnp.zeros((rows, BLK), jnp.float32), unroll=4)
    mean = jnp.sum(acc, axis=1, keepdims=True) * (1.0 / D)
    scale[...] = jnp.broadcast_to(lax.rsqrt(mean + 1e-06), scale.shape)


def sum_sent(sent, sel, rows, D):
    reps = sel.shape[0]
    vmem = pl.BlockSpec(memory_space=pltpu.VMEM)
    return pl.pallas_call(
        functools.partial(sum_sent_kernel, reps),
        out_shape=[
            jax.ShapeDtypeStruct((rows, D), jnp.float32),
            jax.ShapeDtypeStruct((rows, BLK), jnp.float32),
        ],
        in_specs=[vmem, vmem],
        out_specs=[vmem, vmem],
        scratch_shapes=[
            pltpu.VMEM((reps,) + sent.shape, sent.dtype),
            pltpu.SemaphoreType.DMA((reps, 3)),
            pltpu.SemaphoreType.DMA((reps,)),
        ],
        compiler_params=pltpu.CompilerParams(collective_id=0, has_side_effects=True),
        name="sum_sent",
    )(sent, sel)


PIECES = 8


def share_rows_kernel(shards, mine, out, send, recv, local):
    dp, s = lax.axis_index("dp"), lax.axis_index("shard")
    core, far = lax.rem(s, 2), s // 2
    group = shards // 2
    g = lax.rem(dp, 4)
    flip1 = lambda v: v + 1 - 2 * lax.rem(v, 2)
    flip2 = lambda v: v + 2 - 4 * lax.rem(v // 2, 2)
    width = mine.shape[1] // PIECES
    inner, side, deep = {"shard": flip1(s)}, {"dp": flip1(dp)}, {"dp": flip2(dp)}
    outer = [2 * lax.rem(far + k, group) + core for k in range(1, group)]

    barrier = pltpu.get_barrier_semaphore()
    for peer in [inner, side, deep] + [{"shard": o} for o in outer]:
        pl.semaphore_signal(barrier, inc=1, device_id=peer, device_id_type=MESH)
    pl.semaphore_wait(barrier, 3 + len(outer))

    lanes = lambda j: pl.ds(pl.multiple_of(j * width, BLK), width)

    def piece(o, j, way, peer):
        ref = out.at[o, :, lanes(j)]
        return copy_to(ref, ref, send.at[o, j, way], recv.at[o, j], peer)

    def own(j, k):
        return copy_to(
            mine.at[:, lanes(j)], out.at[s, :, lanes(j)], send.at[s, j, k], recv.at[s, j], {"shard": outer[k]}
        )

    sends = []

    def go(c):
        c.start()
        sends.append(c)

    for half in (0, 4):
        for k in range(len(outer)):
            go(own(g + half, k))
    go(copy_to(mine, out.at[s], send.at[s, 0, group], recv.at[s, PIECES], inner))
    keep = pltpu.make_async_copy(mine, out.at[s], local)
    keep.start()

    for half in (0, 4):
        for o in outer:
            j = g + half
            piece(o, j, 0, inner).wait_recv()
            go(piece(o, j, 0, side))
            go(piece(o, j, 1, deep))
            go(piece(o, j, 2, inner))
    a, b, c = flip1(g), flip2(g), flip2(flip1(g))
    for half in (0, 4):
        for o in outer:
            piece(o, a + half, 0, inner).wait_recv()
            if half == 0:
                go(piece(o, a + half, 1, deep))
            go(piece(o, a + half, 2, inner))
            piece(o, b + half, 0, inner).wait_recv()
            if half == 4:
                go(piece(o, b + half, 0, side))
            go(piece(o, b + half, 2, inner))
    for half in (0, 4):
        for o in outer:
            piece(o, c + half, 0, inner).wait_recv()
            go(piece(o, c + half, 2, inner))
    for o in outer:
        for j in range(PIECES):
            piece(flip1(o), j, 0, inner).wait_recv()
    other = flip1(s)
    copy_to(mine, out.at[other], send.at[other, 0, 0], recv.at[other, PIECES], inner).wait_recv()
    for x in sends:
        x.wait_send()
    keep.wait()


def share_rows(copy, shards):
    rows, D = copy.shape
    out = pl.pallas_call(
        functools.partial(share_rows_kernel, shards),
        out_shape=jax.ShapeDtypeStruct((shards, rows, D), copy.dtype),
        in_specs=[pl.BlockSpec(memory_space=pltpu.VMEM)],
        out_specs=pl.BlockSpec(memory_space=pl.ANY),
        scratch_shapes=[
            pltpu.SemaphoreType.DMA((shards, PIECES, max(3, shards))),
            pltpu.SemaphoreType.DMA((shards, PIECES + 1)),
            pltpu.SemaphoreType.DMA,
        ],
        compiler_params=pltpu.CompilerParams(collective_id=1, has_side_effects=True),
        name="share_rows",
    )(copy)
    return out.reshape(shards * rows, D)


def on_device(grads, momentum, param, thresholds, sel_blocks, counts):
    rows, D = param.shape
    width = min(1024, D)
    fwd, inv = (jnp.asarray(t) for t in tables())
    new_momentum, sent = encode(
        momentum[0], grads[0], thresholds[None, :], sel_blocks, counts[:, 0], fwd, inv, width
    )
    total, scale = sum_sent(sent, sel_blocks, rows, D)
    new_param, copy = apply(total, scale, param, inv, width)
    compute_copy = share_rows(copy, lax.axis_size("shard"))
    return (new_momentum[None], new_param, compute_copy)


def solution(mesh):
    placed = (
        P("dp", "shard", None),
        P("dp", "shard", None),
        P("shard", None),
        P("shard"),
        P(None, "shard", None),
        P(None, "shard"),
    )
    return jax.shard_map(
        on_device,
        mesh=mesh,
        in_specs=placed,
        out_specs=(P("dp", "shard", None), P("shard", None), P()),
        check_vma=False,
    )
```

```python
import functools

import jax
import jax.numpy as jnp
import numpy as np
from jax import lax
from jax.experimental import pallas as pl
from jax.experimental.pallas import tpu as pltpu
from jax.sharding import PartitionSpec as P

BLK = 128
HALF = 64
beta_decay = 0.999
step_size = 0.1
UNROLL = 16


def tables():
    pos = np.arange(BLK)
    sample, freq = (pos % HALF)[:, None], (pos % HALF)[None, :]
    same = pos[:, None] // HALF == pos[None, :] // HALF
    weights = np.where(freq == 0, np.sqrt(1.0 / HALF), np.sqrt(2.0 / HALF))
    table = np.where(same, weights * np.cos((2 * sample + 1) * freq * (np.pi / BLK)), 0.0).astype(np.float32)

    def wide(t):
        hi = t.astype(jnp.bfloat16)
        lo = (t - hi.astype(np.float32)).astype(jnp.bfloat16)
        half = np.concatenate([hi, lo], axis=1)
        return np.concatenate([half, half], axis=0)

    return wide(table), wide(table.T)


def split(x):
    hi = x.astype(jnp.bfloat16)
    lo = (x - hi.astype(jnp.float32)).astype(jnp.bfloat16)
    return jnp.concatenate([hi, lo], axis=1)


def both(x, w):
    y = jnp.dot(x, w, preferred_element_type=jnp.float32)
    return y[:, :BLK] + y[:, BLK:]


def tiles(x):
    return jnp.concatenate([x[:, c * BLK : (c + 1) * BLK] for c in range(x.shape[1] // BLK)], axis=0)


def encode_kernel(per_row, mom, grad, thr, sel, place, counts, fwd, inv, newmom, sent, rowhot, dense, picked, level):
    step = pl.program_id(0)
    replica = lax.axis_index("dp")
    rows, width = mom.shape
    slots = sel.shape[2]
    cols = width // BLK
    ids = sel[replica]

    @pl.when(step == 0)
    def _():
        live = lax.broadcasted_iota(jnp.int32, (1, slots), 1) < counts[replica]
        row_of = jnp.where(live, ids // per_row, -1)
        hot = row_of == lax.broadcasted_iota(jnp.int32, (rows, slots), 0)
        rowhot[...] = jnp.where(hot, 1.0, 0.0).astype(jnp.bfloat16)
        eye = lax.broadcasted_iota(jnp.int32, (rows, rows), 0) == lax.broadcasted_iota(jnp.int32, (rows, rows), 1)
        column = jnp.sum(jnp.where(eye, thr[...], 0.0), axis=1, keepdims=True)
        level[...] = jnp.broadcast_to(column, level.shape)

    colhot = ids % per_row == step * cols + lax.broadcasted_iota(jnp.int32, (max(cols, 8), slots), 0)
    mask = lax.dot_general(
        rowhot[...],
        jnp.where(colhot, 1.0, 0.0).astype(jnp.bfloat16),
        (((1,), (1,)), ((), ())),
        preferred_element_type=jnp.float32,
    )
    blended = tiles(beta_decay * mom[...] + grad[...].astype(jnp.float32))
    coef = both(split(blended), fwd[...])
    t = jnp.concatenate([level[...]] * cols, axis=0)
    shrunk = coef - jnp.clip(coef, -t, t)
    keep = jnp.concatenate([jnp.broadcast_to(mask[:, c : c + 1], (rows, BLK)) for c in range(cols)], axis=0)
    kept = jnp.where(keep > 0.5, shrunk, 0.0)
    for c in range(cols):
        dense[pl.ds(step * cols + c, rows, stride=per_row), :] = kept[c * rows : (c + 1) * rows]
    out = blended - both(kept.astype(jnp.bfloat16), inv[:BLK, :])
    for c in range(cols):
        newmom[:, c * BLK : (c + 1) * BLK] = out[c * rows : (c + 1) * rows]

    @pl.when(step == pl.num_programs(0) - 1)
    def _():
        def pick(i, carry):
            base = i * UNROLL
            got = [dense[pl.ds(place[replica, 0, base + u], 1), :] for u in range(UNROLL)]
            for u in range(UNROLL):
                picked[pl.ds(base + u, 1), :] = got[u]
            return carry

        lax.fori_loop(0, slots // UNROLL, pick, 0)
        sent[...] = picked[...].astype(jnp.bfloat16)


def encode(mom, grad, thr, sel, counts, fwd, inv, width):
    rows, D = mom.shape
    slots = sel.shape[2]
    col = pl.BlockSpec((rows, width), lambda i: (0, i))
    whole = lambda a: pl.BlockSpec(a.shape, lambda i: (0,) * a.ndim)
    smem = pl.BlockSpec(memory_space=pltpu.SMEM)
    return pl.pallas_call(
        functools.partial(encode_kernel, D // BLK),
        grid=(D // width,),
        in_specs=[col, col, whole(thr), whole(sel), smem, smem, whole(fwd), whole(inv)],
        out_specs=[col, pl.BlockSpec((slots, BLK), lambda i: (0, 0))],
        out_shape=[
            jax.ShapeDtypeStruct(mom.shape, jnp.float32),
            jax.ShapeDtypeStruct((slots, BLK), jnp.bfloat16),
        ],
        scratch_shapes=[
            pltpu.VMEM((rows, slots), jnp.bfloat16),
            pltpu.VMEM((rows * (D // BLK), BLK), jnp.float32),
            pltpu.VMEM((slots, BLK), jnp.float32),
            pltpu.VMEM((rows, BLK), jnp.float32),
        ],
        name="encode",
    )(mom, grad, thr, sel, sel, counts, fwd, inv)


MESH = pl.DeviceIdType.MESH


def copy_to(src, dst, send, recv, peer):
    return pltpu.make_async_remote_copy(
        src_ref=src, dst_ref=dst, send_sem=send, recv_sem=recv, device_id=peer, device_id_type=MESH
    )


CLASSES = 4
PIECES = 16


def exchange_kernel(
    reps, shards, mine, sel, param, inv, newparam, rowsout, total, scale, pbuf, cbuf, buf, send, recv, send2, recv2, local
):
    fetch = pltpu.make_async_copy(param, pbuf, local.at[0])
    fetch.start()
    s = lax.axis_index("shard")
    group = shards // 2
    core, far = lax.rem(s, 2), s // 2
    flip1 = lambda v: v + 1 - 2 * lax.rem(v, 2)
    flip2 = lambda v: v + 2 - 4 * lax.rem(v // 2, 2)
    inner = {"shard": flip1(s)}
    outer = [2 * lax.rem(far + k, group) + core for k in range(1, group)]

    me = lax.axis_index("dp")
    line, side = me // 2, lax.rem(me, 2)
    length = reps // 2
    rows, D = total.shape
    per_row = D // BLK
    slots = mine.shape[0]
    up, down, across = {"dp": me + 2}, {"dp": me - 2}, {"dp": me + 1 - 2 * side}
    has_up, has_down = line < length - 1, line > 0

    barrier = pltpu.get_barrier_semaphore()
    pl.semaphore_signal(barrier, inc=1, device_id=across, device_id_type=MESH)

    @pl.when(has_up)
    def _():
        pl.semaphore_signal(barrier, inc=1, device_id=up, device_id_type=MESH)

    @pl.when(has_down)
    def _():
        pl.semaphore_signal(barrier, inc=1, device_id=down, device_id_type=MESH)

    for peer in [inner] + [{"shard": o} for o in outer]:
        pl.semaphore_signal(barrier, inc=1, device_id=peer, device_id_type=MESH)
    pl.semaphore_wait(barrier, 2 + len(outer) + jnp.where(has_up, 1, 0) + jnp.where(has_down, 1, 0))

    def block(i, way, peer, own=False):
        src = mine if own else buf.at[i]
        return copy_to(src, buf.at[i], send.at[i, way], recv.at[i], peer)

    def first(act):
        @pl.when(has_up)
        def _():
            getattr(block(me, 0, up, True), act)()

        @pl.when(has_down)
        def _():
            getattr(block(me, 1, down, True), act)()

        getattr(block(me, 2, across, True), act)()

    def relay(d, act):
        @pl.when(line >= d)
        def _():
            i = me - 2 * d
            if act == "start":
                block(i, 0, across).wait_recv()

            @pl.when(has_up)
            def _():
                getattr(block(i, 0, up), act)()

            getattr(block(i, 2, across), act)()

        @pl.when(line + d < length)
        def _():
            i = me + 2 * d
            if act == "start":
                block(i, 1, across).wait_recv()

            @pl.when(has_down)
            def _():
                getattr(block(i, 1, down), act)()

            getattr(block(i, 2, across), act)()

    first("start")
    total[...] = jnp.zeros_like(total)
    batch = min(8, per_row // 2)

    def accumulate(i):
        ids = sel[i]
        col = ids % per_row
        hot = ids // per_row == lax.broadcasted_iota(jnp.int32, (rows, slots), 0)
        rowhot = jnp.where(hot, 1.0, 0.0).astype(jnp.bfloat16)
        odd = jnp.transpose(jnp.broadcast_to((col % 2).astype(jnp.float32), (BLK, slots)))
        right = odd.astype(jnp.bfloat16)
        values = buf[i]
        rhs = jnp.concatenate([values * (1.0 - odd).astype(jnp.bfloat16), values * right], axis=1)
        pair = jnp.broadcast_to(col // 2, (16, slots))

        def chunk(q, carry):
            parts = []
            for u in range(batch):
                pick = jnp.where(pair == q * batch + u, 1.0, 0.0).astype(jnp.bfloat16)
                parts.append(rowhot * jnp.concatenate([pick] * (rows // 16), axis=0))
            out = jnp.dot(jnp.concatenate(parts, axis=0), rhs, preferred_element_type=jnp.float32)
            for u in range(batch):
                at = pl.ds(pl.multiple_of((q * batch + u) * (2 * BLK), BLK), 2 * BLK)
                total[:, at] += out[u * rows : (u + 1) * rows]
            return carry

        lax.fori_loop(0, per_row // 2 // batch, chunk, 0)

    buf[me] = mine[...]

    def step(d, carry):
        @pl.when(d > 0)
        def _():
            relay(d, "start")

        def visit(t, carry):
            other = t // 2
            far = d - other
            at = line + (2 * lax.rem(t, 2) - 1) * far
            twin = (far == 0) & (lax.rem(t, 2) == 1)

            @pl.when((far >= 0) & (at >= 0) & (at < length) & jnp.logical_not(twin))
            def _():
                i = 2 * at + side + other * (1 - 2 * side)

                @pl.when(other == 1)
                def _():
                    block(i, 2, across).wait_recv()

                accumulate(i)

            return carry

        lax.fori_loop(0, 4, visit, 0)
        return carry

    lax.fori_loop(0, length + 1, step, 0)
    def square(c, acc):
        lanes = pl.ds(pl.multiple_of(c * BLK, BLK), BLK)
        a = total[:, lanes] * (1.0 / reps)
        total[:, lanes] = a
        return acc + a * a

    acc = lax.fori_loop(0, per_row, square, jnp.zeros((rows, BLK), jnp.float32), unroll=4)
    mean = jnp.sum(acc, axis=1, keepdims=True) * (1.0 / D)
    scale[...] = jnp.broadcast_to(lax.rsqrt(mean + 1e-06), scale.shape)
    fetch.wait()

    g = lax.rem(me, CLASSES)
    width = D // PIECES
    deep, side_peer = {"dp": flip2(me)}, across
    turns = PIECES // CLASSES

    def lanes(j):
        return pl.ds(pl.multiple_of(j * width, BLK), width)

    def piece(o, j, way, peer):
        ref = rowsout.at[o, :, lanes(j)]
        return copy_to(ref, ref, send2.at[o, j, way], recv2.at[o, j], peer)

    def own(j, k):
        return copy_to(
            cbuf.at[:, lanes(j)], rowsout.at[s, :, lanes(j)], send2.at[s, j, k], recv2.at[s, j], {"shard": outer[k]}
        )

    def compute(j):
        direction = both(split(tiles(total[:, lanes(j)])), inv[...])
        for c in range(width // BLK):
            at = pl.ds(pl.multiple_of(j * width + c * BLK, BLK), BLK)
            update = jnp.tanh(direction[c * rows : (c + 1) * rows] * scale[...])
            new = pbuf[:, at] - step_size * update
            pbuf[:, at] = new
            cbuf[:, at] = new.astype(jnp.bfloat16)

    def lead(k, carry):
        compute(g + CLASSES * k)

        @pl.when(k > 0)
        def _():
            for n in range(len(outer)):
                own(g + CLASSES * (k - 1), n).start()

        return carry

    def rest(turn):
        def one(k, carry):
            compute(lax.rem(g + turn, CLASSES) + CLASSES * k)
            return carry

        lax.fori_loop(0, turns, one, 0)

    sends = []

    def go(c):
        c.start()
        sends.append(c)

    lax.fori_loop(0, turns, lead, 0)
    rest(1)
    for n in range(len(outer)):
        own(g + CLASSES * (turns - 1), n).start()
        sends.extend(own(g + CLASSES * k, n) for k in range(turns))
    for k in range(turns):
        j = g + CLASSES * k
        for o in outer:
            piece(o, j, 0, inner).wait_recv()
            go(piece(o, j, 0, side_peer))
            go(piece(o, j, 1, deep))
            go(piece(o, j, 2, inner))
        if k < 2:
            rest(k + 2)
        if k == 1:
            store = pltpu.make_async_copy(pbuf, newparam, local.at[0])
            store.start()
    go(copy_to(cbuf, rowsout.at[s], send2.at[s, 0, group], recv2.at[s, PIECES], inner))
    keep = pltpu.make_async_copy(cbuf, rowsout.at[s], local.at[1])
    keep.start()
    a, b, c = flip1(g), flip2(g), flip2(flip1(g))
    for k in range(turns):
        for o in outer:
            j = a + CLASSES * k
            piece(o, j, 0, inner).wait_recv()
            if k % 2 == 0:
                go(piece(o, j, 1, deep))
            go(piece(o, j, 2, inner))
            j = b + CLASSES * k
            piece(o, j, 0, inner).wait_recv()
            if k % 2 == 1:
                go(piece(o, j, 0, side_peer))
            go(piece(o, j, 2, inner))
    for k in range(turns):
        for o in outer:
            piece(o, c + CLASSES * k, 0, inner).wait_recv()
            go(piece(o, c + CLASSES * k, 2, inner))
    other = flip1(s)
    copy_to(cbuf, rowsout.at[other], send2.at[other, 0, 0], recv2.at[other, PIECES], inner).wait_recv()
    for o in outer:
        for j in range(PIECES):
            piece(flip1(o), j, 0, inner).wait_recv()
    for x in sends:
        x.wait_send()
    first("wait_send")

    def drain(d, carry):
        relay(d, "wait_send")
        return carry

    lax.fori_loop(1, length, drain, 0)
    store.wait()
    keep.wait()


def exchange(sent, sel, param, inv, shards):
    reps = sel.shape[0]
    rows, D = param.shape
    vmem = pl.BlockSpec(memory_space=pltpu.VMEM)
    hbm = pl.BlockSpec(memory_space=pl.ANY)
    return pl.pallas_call(
        functools.partial(exchange_kernel, reps, shards),
        out_shape=[
            jax.ShapeDtypeStruct((rows, D), jnp.float32),
            jax.ShapeDtypeStruct((shards, rows, D), jnp.bfloat16),
        ],
        in_specs=[vmem, vmem, hbm, vmem],
        out_specs=[hbm, hbm],
        scratch_shapes=[
            pltpu.VMEM((rows, D), jnp.float32),
            pltpu.VMEM((rows, BLK), jnp.float32),
            pltpu.VMEM((rows, D), jnp.float32),
            pltpu.VMEM((rows, D), jnp.bfloat16),
            pltpu.VMEM((reps,) + sent.shape, sent.dtype),
            pltpu.SemaphoreType.DMA((reps, 3)),
            pltpu.SemaphoreType.DMA((reps,)),
            pltpu.SemaphoreType.DMA((shards, PIECES, max(3, shards))),
            pltpu.SemaphoreType.DMA((shards, PIECES + 1)),
            pltpu.SemaphoreType.DMA((2,)),
        ],
        compiler_params=pltpu.CompilerParams(collective_id=0, has_side_effects=True),
        name="exchange",
    )(sent, sel, param, inv)


def on_device(grads, momentum, param, thresholds, sel_blocks, counts):
    rows, D = param.shape
    width = min(1024, D)
    fwd, inv = (jnp.asarray(t) for t in tables())
    new_momentum, sent = encode(
        momentum[0], grads[0], thresholds[None, :], sel_blocks, counts[:, 0], fwd, inv, width
    )
    shards = lax.axis_size("shard")
    new_param, copies = exchange(sent, sel_blocks, param, inv, shards)
    compute_copy = copies.reshape(shards * rows, D)
    return (new_momentum[None], new_param, compute_copy)


def solution(mesh):
    placed = (
        P("dp", "shard", None),
        P("dp", "shard", None),
        P("shard", None),
        P("shard"),
        P(None, "shard", None),
        P(None, "shard"),
    )
    return jax.shard_map(
        on_device,
        mesh=mesh,
        in_specs=placed,
        out_specs=(P("dp", "shard", None), P("shard", None), P()),
        check_vma=False,
    )
```

```python
import functools

import jax
import jax.numpy as jnp
import numpy as np
from jax import lax
from jax.experimental import pallas as pl
from jax.experimental.pallas import tpu as pltpu
from jax.sharding import PartitionSpec as P

BLK = 128
HALF = 64
beta_decay = 0.999
step_size = 0.1
UNROLL = 16


def tables():
    pos = np.arange(BLK)
    sample, freq = (pos % HALF)[:, None], (pos % HALF)[None, :]
    same = pos[:, None] // HALF == pos[None, :] // HALF
    weights = np.where(freq == 0, np.sqrt(1.0 / HALF), np.sqrt(2.0 / HALF))
    table = np.where(same, weights * np.cos((2 * sample + 1) * freq * (np.pi / BLK)), 0.0).astype(np.float32)

    def wide(t):
        hi = t.astype(jnp.bfloat16)
        lo = (t - hi.astype(np.float32)).astype(jnp.bfloat16)
        half = np.concatenate([hi, lo], axis=1)
        return np.concatenate([half, half], axis=0)

    return wide(table), wide(table.T)


def split(x):
    hi = x.astype(jnp.bfloat16)
    lo = (x - hi.astype(jnp.float32)).astype(jnp.bfloat16)
    return jnp.concatenate([hi, lo], axis=1)


def both(x, w):
    y = jnp.dot(x, w, preferred_element_type=jnp.float32)
    return y[:, :BLK] + y[:, BLK:]


def tiles(x):
    return jnp.concatenate([x[:, c * BLK : (c + 1) * BLK] for c in range(x.shape[1] // BLK)], axis=0)


def encode_kernel(per_row, mom, grad, thr, sel, place, counts, fwd, inv, newmom, sent, rowhot, dense, picked, level):
    step = pl.program_id(0)
    replica = lax.axis_index("dp")
    rows, width = mom.shape
    slots = sel.shape[2]
    cols = width // BLK
    ids = sel[replica]

    @pl.when(step == 0)
    def _():
        live = lax.broadcasted_iota(jnp.int32, (1, slots), 1) < counts[replica]
        row_of = jnp.where(live, ids // per_row, -1)
        hot = row_of == lax.broadcasted_iota(jnp.int32, (rows, slots), 0)
        rowhot[...] = jnp.where(hot, 1.0, 0.0).astype(jnp.bfloat16)
        eye = lax.broadcasted_iota(jnp.int32, (rows, rows), 0) == lax.broadcasted_iota(jnp.int32, (rows, rows), 1)
        column = jnp.sum(jnp.where(eye, thr[...], 0.0), axis=1, keepdims=True)
        level[...] = jnp.broadcast_to(column, level.shape)

    colhot = ids % per_row == step * cols + lax.broadcasted_iota(jnp.int32, (max(cols, 8), slots), 0)
    mask = lax.dot_general(
        rowhot[...],
        jnp.where(colhot, 1.0, 0.0).astype(jnp.bfloat16),
        (((1,), (1,)), ((), ())),
        preferred_element_type=jnp.float32,
    )
    blended = tiles(beta_decay * mom[...] + grad[...].astype(jnp.float32))
    coef = both(split(blended), fwd[...])
    t = jnp.concatenate([level[...]] * cols, axis=0)
    shrunk = coef - jnp.clip(coef, -t, t)
    keep = jnp.concatenate([jnp.broadcast_to(mask[:, c : c + 1], (rows, BLK)) for c in range(cols)], axis=0)
    kept = jnp.where(keep > 0.5, shrunk, 0.0)
    for c in range(cols):
        dense[pl.ds(step * cols + c, rows, stride=per_row), :] = kept[c * rows : (c + 1) * rows]
    out = blended - both(kept.astype(jnp.bfloat16), inv[:BLK, :])
    for c in range(cols):
        newmom[:, c * BLK : (c + 1) * BLK] = out[c * rows : (c + 1) * rows]

    @pl.when(step == pl.num_programs(0) - 1)
    def _():
        def pick(i, carry):
            base = i * UNROLL
            got = [dense[pl.ds(place[replica, 0, base + u], 1), :] for u in range(UNROLL)]
            for u in range(UNROLL):
                picked[pl.ds(base + u, 1), :] = got[u]
            return carry

        lax.fori_loop(0, slots // UNROLL, pick, 0)
        sent[...] = picked[...].astype(jnp.bfloat16)


def encode(mom, grad, thr, sel, counts, fwd, inv, width):
    rows, D = mom.shape
    slots = sel.shape[2]
    col = pl.BlockSpec((rows, width), lambda i: (0, i))
    whole = lambda a: pl.BlockSpec(a.shape, lambda i: (0,) * a.ndim)
    smem = pl.BlockSpec(memory_space=pltpu.SMEM)
    return pl.pallas_call(
        functools.partial(encode_kernel, D // BLK),
        grid=(D // width,),
        in_specs=[col, col, whole(thr), whole(sel), smem, smem, whole(fwd), whole(inv)],
        out_specs=[col, pl.BlockSpec((slots, BLK), lambda i: (0, 0))],
        out_shape=[
            jax.ShapeDtypeStruct(mom.shape, jnp.float32),
            jax.ShapeDtypeStruct((slots, BLK), jnp.bfloat16),
        ],
        scratch_shapes=[
            pltpu.VMEM((rows, slots), jnp.bfloat16),
            pltpu.VMEM((rows * (D // BLK), BLK), jnp.float32),
            pltpu.VMEM((slots, BLK), jnp.float32),
            pltpu.VMEM((rows, BLK), jnp.float32),
        ],
        name="encode",
    )(mom, grad, thr, sel, sel, counts, fwd, inv)


MESH = pl.DeviceIdType.MESH


def copy_to(src, dst, send, recv, peer):
    return pltpu.make_async_remote_copy(
        src_ref=src, dst_ref=dst, send_sem=send, recv_sem=recv, device_id=peer, device_id_type=MESH
    )


CLASSES = 4
PIECES = 16


def exchange_kernel(
    reps, shards, mine, sel, param, inv, newparam, rowsout, total, scale, pbuf, cbuf, buf, send, recv, send2, recv2, local
):
    fetch = pltpu.make_async_copy(param, pbuf, local.at[0])
    fetch.start()
    s = lax.axis_index("shard")
    group = shards // 2
    core, far = lax.rem(s, 2), s // 2
    flip1 = lambda v: v + 1 - 2 * lax.rem(v, 2)
    flip2 = lambda v: v + 2 - 4 * lax.rem(v // 2, 2)
    inner = {"shard": flip1(s)}
    outer = [2 * lax.rem(far + k, group) + core for k in range(1, group)]

    me = lax.axis_index("dp")
    line, side = me // 2, lax.rem(me, 2)
    length = reps // 2
    rows, D = total.shape
    per_row = D // BLK
    slots = mine.shape[0]
    up, down, across = {"dp": me + 2}, {"dp": me - 2}, {"dp": me + 1 - 2 * side}
    has_up, has_down = line < length - 1, line > 0

    barrier = pltpu.get_barrier_semaphore()
    pl.semaphore_signal(barrier, inc=1, device_id=across, device_id_type=MESH)

    @pl.when(has_up)
    def _():
        pl.semaphore_signal(barrier, inc=1, device_id=up, device_id_type=MESH)

    @pl.when(has_down)
    def _():
        pl.semaphore_signal(barrier, inc=1, device_id=down, device_id_type=MESH)

    for peer in [inner] + [{"shard": o} for o in outer]:
        pl.semaphore_signal(barrier, inc=1, device_id=peer, device_id_type=MESH)
    pl.semaphore_wait(barrier, 2 + len(outer) + jnp.where(has_up, 1, 0) + jnp.where(has_down, 1, 0))

    def block(i, way, peer, own=False):
        src = mine if own else buf.at[i]
        return copy_to(src, buf.at[i], send.at[i, way], recv.at[i], peer)

    def first(act):
        @pl.when(has_up)
        def _():
            getattr(block(me, 0, up, True), act)()

        @pl.when(has_down)
        def _():
            getattr(block(me, 1, down, True), act)()

        getattr(block(me, 2, across, True), act)()

    def relay(d, act):
        @pl.when(line >= d)
        def _():
            i = me - 2 * d
            if act == "start":
                block(i, 0, across).wait_recv()

            @pl.when(has_up)
            def _():
                getattr(block(i, 0, up), act)()

            getattr(block(i, 2, across), act)()

        @pl.when(line + d < length)
        def _():
            i = me + 2 * d
            if act == "start":
                block(i, 1, across).wait_recv()

            @pl.when(has_down)
            def _():
                getattr(block(i, 1, down), act)()

            getattr(block(i, 2, across), act)()

    first("start")
    total[...] = jnp.zeros_like(total)
    batch = min(8, per_row // 2)

    def accumulate(i):
        ids = sel[i]
        col = ids % per_row
        hot = ids // per_row == lax.broadcasted_iota(jnp.int32, (rows, slots), 0)
        rowhot = jnp.where(hot, 1.0, 0.0).astype(jnp.bfloat16)
        odd = jnp.transpose(jnp.broadcast_to((col % 2).astype(jnp.float32), (BLK, slots)))
        right = odd.astype(jnp.bfloat16)
        values = buf[i]
        rhs = jnp.concatenate([values * (1.0 - odd).astype(jnp.bfloat16), values * right], axis=1)
        pair = jnp.broadcast_to(col // 2, (16, slots))

        def chunk(q, carry):
            parts = []
            for u in range(batch):
                pick = jnp.where(pair == q * batch + u, 1.0, 0.0).astype(jnp.bfloat16)
                parts.append(rowhot * jnp.concatenate([pick] * (rows // 16), axis=0))
            out = jnp.dot(jnp.concatenate(parts, axis=0), rhs, preferred_element_type=jnp.float32)
            for u in range(batch):
                at = pl.ds(pl.multiple_of((q * batch + u) * (2 * BLK), BLK), 2 * BLK)
                total[:, at] += out[u * rows : (u + 1) * rows]
            return carry

        lax.fori_loop(0, per_row // 2 // batch, chunk, 0)

    buf[me] = mine[...]

    def step(d, carry):
        @pl.when(d > 0)
        def _():
            relay(d, "start")

        def visit(t, carry):
            other = t // 2
            far = d - other
            at = line + (2 * lax.rem(t, 2) - 1) * far
            twin = (far == 0) & (lax.rem(t, 2) == 1)

            @pl.when((far >= 0) & (at >= 0) & (at < length) & jnp.logical_not(twin))
            def _():
                i = 2 * at + side + other * (1 - 2 * side)

                @pl.when(other == 1)
                def _():
                    block(i, 2, across).wait_recv()

                accumulate(i)

            return carry

        lax.fori_loop(0, 4, visit, 0)
        return carry

    lax.fori_loop(0, length + 1, step, 0)
    def square(c, acc):
        lanes = pl.ds(pl.multiple_of(c * BLK, BLK), BLK)
        a = total[:, lanes] * (1.0 / reps)
        total[:, lanes] = a
        return acc + a * a

    acc = lax.fori_loop(0, per_row, square, jnp.zeros((rows, BLK), jnp.float32), unroll=4)
    mean = jnp.sum(acc, axis=1, keepdims=True) * (1.0 / D)
    scale[...] = jnp.broadcast_to(lax.rsqrt(mean + 1e-06), scale.shape)
    fetch.wait()

    g = lax.rem(me, CLASSES)
    width = D // PIECES
    deep, side_peer = {"dp": flip2(me)}, across
    turns = PIECES // CLASSES

    def lanes(j):
        return pl.ds(pl.multiple_of(j * width, BLK), width)

    def piece(o, j, way, peer):
        ref = rowsout.at[o, :, lanes(j)]
        return copy_to(ref, ref, send2.at[o, j, way], recv2.at[o, j], peer)

    def own(j, k):
        return copy_to(
            cbuf.at[:, lanes(j)], rowsout.at[s, :, lanes(j)], send2.at[s, j, k], recv2.at[s, j], {"shard": outer[k]}
        )

    def compute(j):
        direction = both(split(tiles(total[:, lanes(j)])), inv[...])
        for c in range(width // BLK):
            at = pl.ds(pl.multiple_of(j * width + c * BLK, BLK), BLK)
            update = jnp.tanh(direction[c * rows : (c + 1) * rows] * scale[...])
            new = pbuf[:, at] - step_size * update
            pbuf[:, at] = new
            cbuf[:, at] = new.astype(jnp.bfloat16)

    def lead(k, carry):
        compute(g + CLASSES * k)

        @pl.when(k > 0)
        def _():
            for n in range(len(outer)):
                own(g + CLASSES * (k - 1), n).start()

        return carry

    def rest(turn):
        def one(k, carry):
            compute(lax.rem(g + turn, CLASSES) + CLASSES * k)
            return carry

        lax.fori_loop(0, turns, one, 0)

    sends = []

    def go(c):
        c.start()
        sends.append(c)

    lax.fori_loop(0, turns, lead, 0)
    rest(1)
    for n in range(len(outer)):
        own(g + CLASSES * (turns - 1), n).start()
        sends.extend(own(g + CLASSES * k, n) for k in range(turns))
    a, b, c = flip1(g), flip2(g), flip2(flip1(g))
    for k in range(turns):
        j = g + CLASSES * k
        for o in outer:
            piece(o, j, 0, inner).wait_recv()
            go(piece(o, j, 0, side_peer))
            go(piece(o, j, 1, deep))
            go(piece(o, j, 2, inner))
        if k < 2:
            rest(k + 2)
        if k == 1:
            store = pltpu.make_async_copy(pbuf, newparam, local.at[0])
            store.start()
        if k == 2:
            for direct in range(2, turns):
                for n in range(len(outer)):
                    go(own(c + CLASSES * direct, n))
    go(copy_to(cbuf, rowsout.at[s], send2.at[s, 0, group], recv2.at[s, PIECES], inner))
    keep = pltpu.make_async_copy(cbuf, rowsout.at[s], local.at[1])
    keep.start()
    for k in range(turns):
        for o in outer:
            j = a + CLASSES * k
            piece(o, j, 0, inner).wait_recv()
            if k == 0:
                go(piece(o, j, 1, deep))
            go(piece(o, j, 2, inner))
            j = b + CLASSES * k
            piece(o, j, 0, inner).wait_recv()
            if k == 1:
                go(piece(o, j, 0, side_peer))
            go(piece(o, j, 2, inner))
    for k in range(turns):
        for o in outer:
            piece(o, c + CLASSES * k, 0, inner).wait_recv()
            go(piece(o, c + CLASSES * k, 2, inner))
    other = flip1(s)
    copy_to(cbuf, rowsout.at[other], send2.at[other, 0, 0], recv2.at[other, PIECES], inner).wait_recv()
    for o in outer:
        for j in range(PIECES):
            piece(flip1(o), j, 0, inner).wait_recv()
    for x in sends:
        x.wait_send()
    first("wait_send")

    def drain(d, carry):
        relay(d, "wait_send")
        return carry

    lax.fori_loop(1, length, drain, 0)
    store.wait()
    keep.wait()


def exchange(sent, sel, param, inv, shards):
    reps = sel.shape[0]
    rows, D = param.shape
    vmem = pl.BlockSpec(memory_space=pltpu.VMEM)
    hbm = pl.BlockSpec(memory_space=pl.ANY)
    return pl.pallas_call(
        functools.partial(exchange_kernel, reps, shards),
        out_shape=[
            jax.ShapeDtypeStruct((rows, D), jnp.float32),
            jax.ShapeDtypeStruct((shards, rows, D), jnp.bfloat16),
        ],
        in_specs=[vmem, vmem, hbm, vmem],
        out_specs=[hbm, hbm],
        scratch_shapes=[
            pltpu.VMEM((rows, D), jnp.float32),
            pltpu.VMEM((rows, BLK), jnp.float32),
            pltpu.VMEM((rows, D), jnp.float32),
            pltpu.VMEM((rows, D), jnp.bfloat16),
            pltpu.VMEM((reps,) + sent.shape, sent.dtype),
            pltpu.SemaphoreType.DMA((reps, 3)),
            pltpu.SemaphoreType.DMA((reps,)),
            pltpu.SemaphoreType.DMA((shards, PIECES, max(3, shards))),
            pltpu.SemaphoreType.DMA((shards, PIECES + 1)),
            pltpu.SemaphoreType.DMA((2,)),
        ],
        compiler_params=pltpu.CompilerParams(collective_id=0, has_side_effects=True),
        name="exchange",
    )(sent, sel, param, inv)


def on_device(grads, momentum, param, thresholds, sel_blocks, counts):
    rows, D = param.shape
    width = min(1024, D)
    fwd, inv = (jnp.asarray(t) for t in tables())
    new_momentum, sent = encode(
        momentum[0], grads[0], thresholds[None, :], sel_blocks, counts[:, 0], fwd, inv, width
    )
    shards = lax.axis_size("shard")
    new_param, copies = exchange(sent, sel_blocks, param, inv, shards)
    compute_copy = copies.reshape(shards * rows, D)
    return (new_momentum[None], new_param, compute_copy)


def solution(mesh):
    placed = (
        P("dp", "shard", None),
        P("dp", "shard", None),
        P("shard", None),
        P("shard"),
        P(None, "shard", None),
        P(None, "shard"),
    )
    return jax.shard_map(
        on_device,
        mesh=mesh,
        in_specs=placed,
        out_specs=(P("dp", "shard", None), P("shard", None), P()),
        check_vma=False,
    )
```
